32 devices in a mesh: groups: 2 (over y), seq: 8 (over z, x), branch: 2 (over core).
Axes of the slice: x: 2, y: 2, z: 4, core: 2. Of those that a mesh axis runs over, the one named last changes fastest.
Arguments:
- queries: bfloat16 [2, 256, 1536], P('branch', ('groups', 'seq')), parts along dimension 1, may hold values from -8 to 8
- key_rows: bfloat16 [2, 256, 1536], P('branch', ('groups', 'seq')), parts along dimension 1, may hold values from -8 to 8
- value_rows: bfloat16 [2, 256, 1536], P('branch', ('groups', 'seq')), parts along dimension 1, may hold values from -40 to 40
- counts: int32 [16], P('groups'), parts along dimension 0, may hold values from 1 to 16, 112 in all
- head_of: int32 [8, 2], replicated, may hold values from 0 to 11, as said below
- out_weight: bfloat16 [1536, 1536], P(None, 'branch'), may hold values from -0.15625 to 0.15625
Outputs:
- projected: bfloat16 [256, 1536], P(('groups', 'seq'), 'branch'), parts along dimension 0
- saved_logsumexp: float32 [2, 16, 2, 16, 8], P('branch', ('groups', 'seq')), parts along dimension 1
The draws below stay inside these ranges and needn't reach their ends.
There are 2 independent parts, one for each index of `groups`. The reference program is written for one: setup_inputs(seed, part) draws one part's arguments, and reference() takes and returns one part's arrays. A program takes and returns all parts, laid end to end along the dimension named above; an argument that names none is the same for every part. Nothing has to cross between parts.
Inputs may be any that keep to these rules, and one draw needn't show every extreme that they name: `head_of`: each of the 12 heads is named by at least 1 entries, and one head by exactly 1.
All inputs are finite; a program needn't handle non-finite values. Where the reference program divides by a largest or mean magnitude, that divisor is 1e-20 or more.
Results may differ from the reference program's by a relative error of at most 0.0063.
Values may be sent and summed in bfloat16 or wider, within the bound.
A program may use at most 64 MiB of HBM per device.

```python
import math
import jax
import jax.numpy as jnp
import numpy as np
from jax import lax

HEADS = 12
HDIM = 128
DOUT = 1536
TOK_DEV = 16
TOKENS = 128
VALID = 112
HSLOT = 2
MINSERVE = 1
QROWS = 16
N_SEQ = 8


def draw_pair(key):
    seed_query = jax.random.fold_in(key, 101)
    seed_keys = jax.random.fold_in(key, 102)
    dims_all = (2, TOKENS, HEADS * HDIM)
    query_draw = jnp.clip(jax.random.normal(seed_query, dims_all, jnp.float32), -8.0, 8.0)
    keys_draw = jnp.clip(jax.random.normal(seed_keys, dims_all, jnp.float32), -8.0, 8.0)
    return (query_draw, keys_draw)


def draw_queries(key, part):
    return draw_pair(key)[0].astype(jnp.bfloat16)


def draw_key_rows(key, part):
    return draw_pair(key)[1].astype(jnp.bfloat16)


def draw_value_rows(key, part):
    seed_base = jax.random.fold_in(key, 201)
    seed_scale = jax.random.fold_in(key, 202)
    column_scale = jnp.exp(jax.random.uniform(seed_scale, (HEADS * HDIM,), jnp.float32, 0.0, math.log(10.0)))
    base_draw = jax.random.normal(seed_base, (2, TOKENS, HEADS * HDIM), jnp.float32)
    return jnp.clip(base_draw * column_scale[None, None, :], -40.0, 40.0).astype(jnp.bfloat16)


def draw_head_of(key, part):
    slot_total = N_SEQ * HSLOT
    spare = slot_total - HEADS * MINSERVE
    seed_lean = jax.random.fold_in(key, 301)
    seed_pick = jax.random.fold_in(key, 302)
    seed_perm = jax.random.fold_in(key, 303)
    lean_head = jax.random.randint(seed_lean, (), 0, HEADS)
    base_rows = jnp.repeat(jnp.arange(HEADS, dtype=jnp.int32), MINSERVE)
    picked = jax.random.randint(seed_pick, (spare,), 0, HEADS - 1)
    picked = picked + (picked >= lean_head).astype(jnp.int32)
    serving = jnp.concatenate([base_rows, picked.astype(jnp.int32)])
    serving = jax.random.permutation(seed_perm, serving)
    return serving.reshape(N_SEQ, HSLOT).astype(jnp.int32)


def levels(stream_key, dims, split, smallest, high):
    loudness = 1.0
    for axis_at, parts in split:
        draws = jax.random.uniform(jax.random.fold_in(jax.random.fold_in(stream_key, 6), axis_at), (parts,), jnp.float32, smallest / len(split), high / len(split))
        loudness = loudness * jnp.repeat(jnp.exp(draws), dims[axis_at] // parts).reshape((-1,) + (1,) * (len(dims) - 1 - axis_at))
    return loudness


def profile(count, total, limit, slope):
    weights = [(1 << 20) // math.isqrt(rank ** slope) + 1 for rank in range(2, count + 1)]
    spare, given = total - limit - (count - 1), [1] * (count - 1)
    while spare > 0:
        free = [i for i in range(count - 1) if given[i] < limit]
        mass, budget = sum([weights[i] for i in free]), spare
        for i in free:
            more = min(limit - given[i], max(1, budget * weights[i] // mass), spare)
            given[i] = given[i] + more
            spare = spare - more
    return np.array([limit] + given)


def uneven_parts(own_key, number_of, total, bound, skew):
    if number_of == 2:
        one = jax.random.randint(own_key, (), max(1, total - bound), min(bound, total - 1) + 1)
        return jnp.stack([one, total - one])
    sizes = jnp.asarray(profile(number_of, total, bound, skew), jnp.int32)
    couples = (number_of - 1) // 2
    giver, sink = sizes[1:1 + 2 * couples:2], sizes[2:2 + 2 * couples:2]
    margin = jnp.minimum(giver - 1, bound - sink)
    shifted = jax.random.randint(jax.random.fold_in(own_key, 1), (couples,), 0, 1 << 20) % (margin + 1)
    sizes = sizes.at[1:1 + 2 * couples:2].set(giver - shifted).at[2:2 + 2 * couples:2].set(sink + shifted)
    return sizes[jax.random.permutation(jax.random.fold_in(own_key, 2), number_of)]


def centred(key, dims, deviation, most, cuts=(), held_as=jnp.bfloat16):
    factor_of = levels(key, dims, cuts, -0.22, 0.18) if cuts else 1.0
    entries = jax.random.normal(key, dims, jnp.float32) * deviation * factor_of
    return jnp.minimum(jnp.maximum(entries, -most), most).astype(held_as)


def setup_inputs(seed: int = 0, part: int = 0) -> dict:
    streams_of = jax.random.split(jax.random.key(seed), 7)
    part_keys = jax.random.split(jax.random.fold_in(streams_of[6], part), 7)
    queries = draw_queries(jax.random.fold_in(jax.random.fold_in(streams_of[6], part), 71), part)
    key_rows = draw_key_rows(jax.random.fold_in(jax.random.fold_in(streams_of[6], part), 71), part)
    value_rows = draw_value_rows(jax.random.fold_in(jax.random.fold_in(streams_of[6], part), 71), part)
    counts = uneven_parts(part_keys[3], N_SEQ, VALID, TOK_DEV, 2).astype(jnp.int32)
    head_of = draw_head_of(jax.random.fold_in(streams_of[6], 71), part)
    out_weight = centred(streams_of[5], (HEADS * HDIM, DOUT), (HEADS * HDIM) ** -0.5, 0.15625, ((1, 2),))
    return dict(queries=queries, key_rows=key_rows, value_rows=value_rows, counts=counts, head_of=head_of, out_weight=out_weight)


GUIDE_SCALE = 3.0
EPSILON = 1e-06

def slot_layout(head_of):
    flat_heads = head_of.reshape(-1)
    slot_order = jnp.arange(flat_heads.shape[0], dtype=jnp.int32)
    same_head = flat_heads[:, None] == flat_heads[None, :]
    group_size = lax.optimization_barrier(jnp.sum(same_head.astype(jnp.int32), axis=1))
    earlier = same_head & (slot_order[None, :] < slot_order[:, None])
    group_rank = lax.optimization_barrier(jnp.sum(earlier.astype(jnp.int32), axis=1))
    return (flat_heads, group_size, group_rank)

def branch_attention(query_all, key_all, value_all, key_valid):
    scale_factor = 1.0 / math.sqrt(HDIM)
    key_float = key_all.reshape(TOKENS, HEADS, HDIM).astype(jnp.float32)
    value_float = value_all.reshape(TOKENS, HEADS, HDIM).astype(jnp.float32)
    query_tiles = query_all.reshape(N_SEQ, TOK_DEV, HEADS, HDIM)

    def one_tile(query_tile):
        scores = jnp.einsum('qhd,khd->hqk', query_tile.astype(jnp.float32), key_float) * scale_factor
        scores = jnp.where(key_valid[None, None, :], scores, -jnp.inf)
        top_score = lax.optimization_barrier(jnp.max(scores, axis=2, keepdims=True))
        weights = jnp.exp(scores - top_score)
        weight_sum = lax.optimization_barrier(jnp.sum(weights, axis=2))
        rounded = lax.optimization_barrier(weights.astype(jnp.bfloat16))
        mixed = jnp.einsum('hqk,khd->qhd', rounded.astype(jnp.float32), value_float)
        attended = mixed / jnp.transpose(weight_sum)[:, :, None]
        logsum = top_score[:, :, 0] + jnp.log(weight_sum)
        return (attended, logsum)
    return lax.map(one_tile, query_tiles)

def reference(queries, key_rows, value_rows, counts, head_of, out_weight):
    positions = jnp.arange(TOK_DEV, dtype=jnp.int32)
    valid_grid = positions[None, :] < counts[:, None]
    key_valid = valid_grid.reshape(-1)
    flat_heads, group_size, group_rank = slot_layout(head_of)
    row_steps = jnp.arange(QROWS, dtype=jnp.int32)
    served_rows = group_rank[:, None] + group_size[:, None] * row_steps[None, :]
    served_ok = served_rows[:, :, None] < counts[None, None, :]
    clipped = jnp.minimum(served_rows, TOK_DEV - 1)
    attended_all = []
    saved_all = []
    for branch_id in range(2):
        attended, logsum = branch_attention(queries[branch_id], key_rows[branch_id], value_rows[branch_id], key_valid)
        attended = jnp.where(valid_grid[:, :, None, None], attended, 0.0)
        attended_all.append(attended.reshape(TOKENS, HEADS * HDIM).astype(jnp.bfloat16))
        by_head = jnp.transpose(logsum, (1, 2, 0))
        picked = by_head[flat_heads[:, None], clipped]
        saved_rows = jnp.where(served_ok, picked, 0.0).reshape(N_SEQ, HSLOT, QROWS, N_SEQ)
        saved_all.append(saved_rows)
    positive = lax.optimization_barrier(attended_all[0]).astype(jnp.float32)
    negative = lax.optimization_barrier(attended_all[1]).astype(jnp.float32)
    guided = GUIDE_SCALE * positive - (GUIDE_SCALE - 1.0) * negative
    magnitude = lax.optimization_barrier(jnp.mean(jnp.abs(guided), axis=1, keepdims=True))
    normed = (guided / (magnitude + EPSILON)).astype(jnp.bfloat16)
    projected = jnp.dot(normed, out_weight, preferred_element_type=jnp.float32).astype(jnp.bfloat16)
    return (projected, jnp.stack(saved_all))
```

```python
import functools
import math

import jax
import jax.numpy as jnp
from jax import lax
from jax.experimental import pallas as pl
from jax.experimental.pallas import tpu as pltpu
from jax.sharding import PartitionSpec as P

HEADS = 12
HDIM = 128


GUIDE_SCALE = 3.0
EPSILON = 1e-06


def partner_2(array, axis, stride):
    return lax.ppermute(array, axis, [(i, i ^ 1 << stride) for i in range(lax.axis_size(axis))])


def slot_layout(head_of):
    flat_heads = head_of.reshape(-1)
    slot_order = jnp.arange(flat_heads.shape[0], dtype=jnp.int32)
    same_head = flat_heads[:, None] == flat_heads[None, :]
    group_size = jnp.sum(same_head.astype(jnp.int32), axis=1)
    earlier = same_head & (slot_order[None, :] < slot_order[:, None])
    group_rank = jnp.sum(earlier.astype(jnp.int32), axis=1)
    return (flat_heads, group_size, group_rank)


def key_grouping(seq_count, tok_dev):
    shard_limit = max(1, 2048 // tok_dev)
    grouping = 1
    for attempt in range(16):
        if grouping * 2 <= shard_limit and seq_count % (grouping * 2) == 0:
            grouping = grouping * 2
    return grouping


def attend_rows(query_block, key_slot, value_slot, key_valid, key_block):
    row_count = query_block.shape[0]
    head_size = query_block.shape[1]
    block_count = key_slot.shape[0] // key_block
    scale_factor = 1.0 / math.sqrt(head_size)

    def fold_block(block_id, state_in):
        top_score, weight_sum, summed = state_in
        scores = (
            jnp.einsum("qd,kd->qk", query_block, key_slot, preferred_element_type=jnp.float32)
            * scale_factor
        )
        scores = jnp.where(key_valid[None, :], scores, -jnp.inf)
        new_top = jnp.maximum(top_score, jnp.max(scores, axis=1))
        fading = jnp.exp(top_score - new_top)
        weights = jnp.exp(scores - new_top[:, None])
        weight_sum = weight_sum * fading + jnp.sum(weights, axis=1)
        summed = summed * fading[:, None] + jnp.dot(
            weights.astype(jnp.bfloat16), value_slot, preferred_element_type=jnp.float32
        )
        return (new_top, weight_sum, summed)

    start_state = (
        jnp.full((row_count,), -jnp.inf, jnp.float32),
        jnp.zeros((row_count,), jnp.float32),
        jnp.zeros((row_count, head_size), jnp.float32),
    )
    top_score, weight_sum, summed = lax.fori_loop(0, block_count, fold_block, start_state)
    return (summed / weight_sum[:, None], top_score + jnp.log(weight_sum))


def serve_slots(query_items, mask_items, key_recv, value_recv, key_valid, key_block):
    source_count, slot_count, item_count, head_size = query_items.shape
    all_tokens = key_recv.shape[0] * key_recv.shape[2]
    per_block = max(1, 512 // source_count)
    slot_outputs = []
    slot_logsum = []
    for slot_id in range(slot_count):
        key_slot = key_recv[:, slot_id].reshape(all_tokens, head_size)
        value_slot = value_recv[:, slot_id].reshape(all_tokens, head_size)
        taken_items = min(per_block, item_count)
        query_block = query_items[:, slot_id, 0:taken_items].reshape(
            source_count * taken_items, head_size
        )
        attended, logsum = attend_rows(query_block, key_slot, value_slot, key_valid, key_block)
        pieces_out = attended.reshape(source_count, taken_items, head_size)
        pieces_sum = logsum.reshape(source_count, taken_items)
        slot_outputs.append(pieces_out)
        slot_logsum.append(pieces_sum)
    attended = jnp.stack(slot_outputs, axis=1)
    logsum = jnp.stack(slot_logsum, axis=1)
    keep_rows = mask_items > 0
    attended = jnp.where(keep_rows[:, :, :, None], attended, 0.0).astype(jnp.bfloat16)
    logsum = jnp.where(keep_rows, logsum, 0.0)
    return (attended, logsum)


def per_device(queries, key_rows, value_rows, counts, head_of, out_weight):
    seq_count = lax.axis_size("seq")
    tok_dev = queries.shape[1]
    slot_count = head_of.shape[1]
    fewest = max(1, seq_count * slot_count // (2 * HEADS))
    row_cap = (tok_dev + fewest - 1) // fewest
    my_index = lax.axis_index("seq")
    flat_heads, group_size, group_rank = slot_layout(head_of)
    row_steps = jnp.arange(row_cap, dtype=jnp.int32)
    served_rows = group_rank[:, None] + group_size[:, None] * row_steps[None, :]
    my_count = counts[my_index]
    clipped = jnp.minimum(served_rows, tok_dev - 1)
    query_grid = queries[0].reshape(tok_dev, HEADS, HDIM)
    row_live = served_rows < my_count
    query_send = query_grid[clipped, flat_heads[:, None]]
    query_send = jnp.where(row_live[:, :, None], query_send, jnp.zeros((), jnp.bfloat16)).reshape(
        seq_count, slot_count, row_cap, HDIM
    )
    mask_send = row_live.astype(jnp.bfloat16).reshape(seq_count, slot_count, row_cap)
    token_ids = jnp.arange(tok_dev, dtype=jnp.int32)
    key_grid = key_rows[0].reshape(tok_dev, HEADS, HDIM)
    value_grid = value_rows[0].reshape(tok_dev, HEADS, HDIM)
    key_send = key_grid[token_ids[None, :], flat_heads[:, None]].reshape(
        seq_count, slot_count, tok_dev, HDIM
    )
    value_send = value_grid[token_ids[None, :], flat_heads[:, None]].reshape(
        seq_count, slot_count, tok_dev, HDIM
    )
    key_valid = (token_ids[None, :] < counts[:, None]).reshape(-1)
    key_block = tok_dev * key_grouping(seq_count, tok_dev)
    query_recv, mask_recv, key_recv, value_recv = (
        lax.all_to_all(query_send, "seq", split_axis=0, concat_axis=0, tiled=True),
        lax.all_to_all(mask_send, "seq", split_axis=0, concat_axis=0, tiled=True),
        lax.all_to_all(key_send, "seq", split_axis=0, concat_axis=0, tiled=True),
        lax.all_to_all(value_send, "seq", split_axis=0, concat_axis=0, tiled=True),
    )
    attended, logsum = serve_slots(
        query_recv, mask_recv, key_recv, value_recv, key_valid, key_block
    )
    returned = lax.all_to_all(attended, "seq", split_axis=0, concat_axis=0, tiled=True)
    head_ids = jnp.arange(HEADS, dtype=jnp.int32)
    head_group = jnp.sum((flat_heads[None, :] == head_ids[:, None]).astype(jnp.int32), axis=1)
    row_rank = token_ids[:, None] % head_group[None, :]
    row_step = token_ids[:, None] // head_group[None, :]
    slot_ids = jnp.arange(flat_heads.shape[0], dtype=jnp.int32)
    matched = (flat_heads[None, None, :] == head_ids[None, :, None]) & (
        group_rank[None, None, :] == row_rank[:, :, None]
    )
    owner_slot = jnp.sum(jnp.where(matched, slot_ids[None, None, :], 0), axis=2)
    flat_index = owner_slot * row_cap + row_step
    returned_rows = returned.reshape(-1, HDIM)
    attended_home = returned_rows[flat_index].reshape(tok_dev, HEADS * HDIM)
    partner = partner_2(attended_home, "branch", 0)
    on_positive = lax.axis_index("branch") == 0
    own_value = attended_home.astype(jnp.float32)
    partner_value = partner.astype(jnp.float32)
    positive = jnp.where(on_positive, own_value, partner_value)
    negative = jnp.where(on_positive, partner_value, own_value)
    guided = GUIDE_SCALE * positive - (GUIDE_SCALE - 1.0) * negative
    magnitude = jnp.mean(jnp.abs(guided), axis=1, keepdims=True)
    normed = (guided / (magnitude + EPSILON)).astype(jnp.bfloat16)
    projected = jnp.dot(normed, out_weight, preferred_element_type=jnp.float32).astype(jnp.bfloat16)
    saved_rows = jnp.transpose(logsum, (1, 2, 0)).reshape(1, 1, slot_count, row_cap, seq_count)
    return (projected, saved_rows)


MESH = pl.DeviceIdType.MESH
LANES = 128


def owner_layout(seq_count, branches):
    chips = max(1, seq_count // 2)
    owners = chips * branches
    return chips, (seq_count - chips) // 2, owners, -(-HEADS // owners)


def fused_kernel(
    seq_count,
    branches,
    counts_hbm,
    heads_hbm,
    query_ref,
    key_ref,
    value_ref,
    weight_ref,
    out_ref,
    saved_ref,
    counts_ref,
    heads_ref,
    query_buf,
    key_buf,
    value_buf,
    weight_buf,
    pack,
    landed,
    bias,
    guided_send,
    lse_send,
    guided_recv,
    lse_recv,
    table_sem,
    load_sem,
    weight_sem,
    send_sem,
    recv_sem,
    gsend_sem,
    grecv_sem,
    lsend_sem,
    lrecv_sem,
):
    seq = lax.axis_index("seq")
    branch = lax.axis_index("branch")
    tok = query_buf.shape[0]
    tokens = seq_count * tok
    slot_count = heads_ref.shape[0]
    me = seq * branches + branch
    everyone = seq_count * branches
    chips, first_chip, owner_count, depth = owner_layout(seq_count, branches)
    is_owner = (seq >= first_chip) & (seq < first_chip + chips)
    my_place = branch * chips + seq - first_chip

    def owner_of(head):
        place = head % owner_count
        return first_chip + place % chips, place // chips

    def not_mine(head):
        owner_seq, owner_branch = owner_of(head)
        return me != owner_seq * branches + owner_branch

    upper = seq // (seq_count // 2)

    def farthest(step):
        at_seq, at_branch = step // branches, step % branches
        return (upper * at_seq + (1 - upper) * (seq_count - 1 - at_seq)) * branches + at_branch

    def heads_by_distance(nearest):
        order = []
        for step in range(chips):
            k = chips - 1 - step if nearest else step
            chip = upper * k + (1 - upper) * (chips - 1 - k)
            for place in range(0, HEADS, chips):
                order.append(chip + place)
        return order

    loads = []
    for at, (src, dst) in enumerate(
        ((query_ref, query_buf), (key_ref, key_buf), (value_ref, value_buf))
    ):
        loads.append(pltpu.make_async_copy(src.at[0], dst, load_sem.at[at]))
        loads[-1].start()
    barrier = pltpu.get_barrier_semaphore()

    def greet(peer):
        pl.semaphore_signal(
            barrier,
            inc=1,
            device_id={"seq": peer // branches, "branch": lax.rem(peer, branches)},
            device_id_type=MESH,
        )

    for step in range(everyone):
        peer = farthest(step)

        @pl.when((peer != me) & is_owner)
        def _():
            greet(peer)

    tables = []
    for at, (src, dst) in enumerate(((counts_hbm, counts_ref), (heads_hbm, heads_ref))):
        tables.append(pltpu.make_async_copy(src, dst, table_sem.at[at]))
        tables[-1].start()
    weight_load = pltpu.make_async_copy(weight_ref, weight_buf, weight_sem)

    for load in loads:
        load.wait()
    for head in range(HEADS):
        columns = slice(head * HDIM, (head + 1) * HDIM)
        pack[head, 0:tok, :] = query_buf[:, columns]
        pack[head, tok : 2 * tok, :] = key_buf[:, columns]
        pack[head, 2 * tok : 3 * tok, :] = value_buf[:, columns]

    @pl.when(is_owner)
    def _():
        pl.semaphore_wait(barrier, owner_count - 1)

    @pl.when(jnp.logical_not(is_owner))
    def _():
        pl.semaphore_wait(barrier, owner_count)

    def block_send(head):
        owner_seq, owner_branch = owner_of(head)
        turn = head // owner_count
        return pltpu.make_async_remote_copy(
            src_ref=pack.at[head],
            dst_ref=landed.at[turn, branch, seq],
            send_sem=send_sem.at[head],
            recv_sem=recv_sem.at[turn, branch, seq],
            device_id={"seq": owner_seq, "branch": owner_branch},
            device_id_type=MESH,
        )

    far = heads_by_distance(False)
    for head in [far[i] for i in range(HEADS) if i % 3 < 2] + [far[i] for i in range(HEADS) if i % 3 == 2]:

        @pl.when(not_mine(head))
        def _():
            block_send(head).start()

    weight_load.start()
    for table in tables:
        table.wait()
    key_shard = lax.broadcasted_iota(jnp.int32, (tokens, tokens), 0)
    limit = jnp.zeros((tokens, tokens), jnp.int32)
    for shard in range(seq_count):
        limit = jnp.where(key_shard // tok == shard, counts_ref[shard], limit)
    bias[...] = jnp.where(key_shard % tok < limit, 0.0, -jnp.inf)

    def attend(turn, which):
        query = landed[turn, which, :, 0:tok, :].reshape(tokens, HDIM)
        key = landed[turn, which, :, tok : 2 * tok, :].reshape(tokens, HDIM)
        value = landed[turn, which, :, 2 * tok : 3 * tok, :].reshape(tokens, HDIM)
        scores = lax.dot_general(
            key, query, (((1,), (1,)), ((), ())), preferred_element_type=jnp.float32
        ) * (1.0 / math.sqrt(HDIM))
        scores = scores + bias[...]
        top = jnp.max(scores, axis=0, keepdims=True)
        weights = jnp.exp(scores - top)
        weight_sum = jnp.sum(weights, axis=0, keepdims=True)
        mixed = lax.dot_general(
            value,
            weights.astype(jnp.bfloat16),
            (((0,), (0,)), ((), ())),
            preferred_element_type=jnp.float32,
        )
        lse_send[turn, which] = top + jnp.log(weight_sum)
        return (mixed / weight_sum).astype(jnp.bfloat16).astype(jnp.float32)

    def answer(head, turn, peer_seq, peer_branch):
        peer = {"seq": peer_seq, "branch": peer_branch}
        at = peer_seq * branches + peer_branch
        return (
            pltpu.make_async_remote_copy(
                src_ref=guided_send.at[turn, peer_seq],
                dst_ref=guided_recv.at[head],
                send_sem=gsend_sem.at[turn, at],
                recv_sem=grecv_sem.at[head],
                device_id=peer,
                device_id_type=MESH,
            ),
            pltpu.make_async_remote_copy(
                src_ref=lse_send.at[turn, peer_branch],
                dst_ref=lse_recv.at[head],
                send_sem=lsend_sem.at[turn, at],
                recv_sem=lrecv_sem.at[head],
                device_id=peer,
                device_id_type=MESH,
            ),
        )

    for turn in range(depth):
        my_head = my_place + turn * owner_count

        @pl.when(is_owner & (my_head < HEADS))
        def _():
            landed[turn, branch, seq] = pack[my_head]
            for peer_branch in range(branches):
                for peer_seq in range(seq_count):

                    @pl.when(me != peer_seq * branches + peer_branch)
                    def _():
                        pltpu.make_async_remote_copy(
                            src_ref=pack.at[0],
                            dst_ref=landed.at[turn, peer_branch, peer_seq],
                            send_sem=send_sem.at[0],
                            recv_sem=recv_sem.at[turn, peer_branch, peer_seq],
                            device_id={"seq": peer_seq, "branch": peer_branch},
                            device_id_type=MESH,
                        ).wait_recv()

            guided = GUIDE_SCALE * attend(turn, 0) - (GUIDE_SCALE - 1.0) * attend(turn, 1)
            guided = guided.T.astype(jnp.bfloat16)
            guided_send[turn] = guided.reshape(seq_count, tok, HDIM)
            for peer in range(everyone):

                @pl.when(peer != me)
                def _():
                    for copy in answer(my_head, turn, peer // branches, peer % branches):
                        copy.start()

            guided_recv[my_head] = guided_send[turn, seq]
            lse_recv[my_head] = lse_send[turn, branch]

    weight_load.wait()
    magnitude = jnp.zeros((tok, 1), jnp.float32)
    projected = jnp.zeros(out_ref.shape, jnp.float32)
    alive = lax.broadcasted_iota(jnp.int32, (tok, 1), 0) < counts_ref[seq]
    order = heads_by_distance(True)
    for first in range(0, HEADS, 2):
        pieces, rows = [], []
        for head in order[first : first + 2]:

            @pl.when(not_mine(head))
            def _():
                answer(head, 0, 0, 0)[0].wait_recv()

            pieces.append(guided_recv[head])
            rows.append(weight_buf[pl.ds(pl.multiple_of(head * HDIM, HDIM), HDIM), :])
        block = jnp.concatenate(pieces, axis=1)
        magnitude += jnp.sum(jnp.abs(block.astype(jnp.float32)), axis=1, keepdims=True)
        projected += jnp.dot(
            block, jnp.concatenate(rows, axis=0), preferred_element_type=jnp.float32
        )
    divisor = magnitude / (HEADS * HDIM) + EPSILON
    out_ref[...] = jnp.where(alive, projected / divisor, 0.0).astype(jnp.bfloat16)

    for head in range(HEADS):

        @pl.when(not_mine(head))
        def _():
            answer(head, 0, 0, 0)[1].wait_recv()

    row_cap = saved_ref.shape[2]
    lane = lax.broadcasted_iota(jnp.int32, (row_cap, tokens), 1)
    row_step = lax.broadcasted_iota(jnp.int32, (row_cap, tokens), 0)
    lane_limit = jnp.zeros((row_cap, tokens), jnp.int32)
    for shard in range(seq_count):
        lane_limit = jnp.where(lane // tok == shard, counts_ref[shard], lane_limit)
    token = lane % tok
    gather = (
        lax.broadcasted_iota(jnp.int32, (seq_count, tokens), 1) // tok
        == lax.broadcasted_iota(jnp.int32, (seq_count, tokens), 0)
    ).astype(jnp.float32)
    for slot in range(slot_count):
        served = heads_ref[slot, seq]
        group = jnp.int32(0)
        rank = jnp.int32(0)
        for other_seq in range(seq_count):
            for other_slot in range(slot_count):
                same = (heads_ref[other_slot, other_seq] == served).astype(jnp.int32)
                earlier = (other_seq * slot_count + other_slot < seq * slot_count + slot).astype(
                    jnp.int32
                )
                group = group + same
                rank = rank + same * earlier
        taken = (token == rank + group * row_step) & (token < lane_limit)
        spread = jnp.where(taken, lse_recv[served], 0.0)
        saved_ref[slot] = lax.dot_general(
            gather,
            spread,
            (((1,), (1,)), ((), ())),
            preferred_element_type=jnp.float32,
            precision=lax.Precision.HIGHEST,
        )

    for head in range(HEADS):

        @pl.when(not_mine(head))
        def _():
            block_send(head).wait_send()

    for turn in range(depth):
        my_head = my_place + turn * owner_count

        @pl.when(is_owner & (my_head < HEADS))
        def _():
            for step in range(everyone):

                @pl.when(me != step)
                def _():
                    for copy in answer(my_head, turn, step // branches, step % branches):
                        copy.wait_send()


def hand_over(projected_ref, saved_ref, projected_out, saved_out):
    projected_out[...] = projected_ref[...]
    saved_out[...] = saved_ref[...]


def fused(seq_count, branches, queries, key_rows, value_rows, counts, head_of, out_weight):
    tok = queries.shape[1]
    slot_count = head_of.shape[1]
    fewest = max(1, seq_count * slot_count // (2 * HEADS))
    row_cap = (tok + fewest - 1) // fewest
    width = queries.shape[2]
    everyone = seq_count * branches
    depth = owner_layout(seq_count, branches)[3]
    dma = pltpu.SemaphoreType.DMA
    anywhere = pl.BlockSpec(memory_space=pl.ANY)
    vmem = pl.BlockSpec(memory_space=pltpu.VMEM)
    projected, saved_rows = pl.pallas_call(
        functools.partial(fused_kernel, seq_count, branches),
        out_shape=(
            pltpu.VMEM((tok, out_weight.shape[1]), jnp.bfloat16),
            pltpu.VMEM((slot_count, seq_count, row_cap), jnp.float32),
        ),
        in_specs=[anywhere, anywhere, anywhere, anywhere, anywhere, anywhere],
        out_specs=(vmem, vmem),
        scratch_shapes=[
            pltpu.SMEM(counts.shape, jnp.int32),
            pltpu.SMEM((slot_count, seq_count), jnp.int32),
            pltpu.VMEM((tok, width), jnp.bfloat16),
            pltpu.VMEM((tok, width), jnp.bfloat16),
            pltpu.VMEM((tok, width), jnp.bfloat16),
            pltpu.VMEM(out_weight.shape, jnp.bfloat16),
            pltpu.VMEM((HEADS, 3 * tok, HDIM), jnp.bfloat16),
            pltpu.VMEM((depth, branches, seq_count, 3 * tok, HDIM), jnp.bfloat16),
            pltpu.VMEM((seq_count * tok, seq_count * tok), jnp.float32),
            pltpu.VMEM((depth, seq_count, tok, HDIM), jnp.bfloat16),
            pltpu.VMEM((depth, branches, 1, seq_count * tok), jnp.float32),
            pltpu.VMEM((HEADS, tok, HDIM), jnp.bfloat16),
            pltpu.VMEM((HEADS, 1, seq_count * tok), jnp.float32),
            dma((2,)),
            dma((3,)),
            dma,
            dma((HEADS,)),
            dma((depth, branches, seq_count)),
            dma((depth, everyone)),
            dma((HEADS,)),
            dma((depth, everyone)),
            dma((HEADS,)),
        ],
        compiler_params=pltpu.CompilerParams(collective_id=0, has_side_effects=True),
        name="guided_attention",
    )(counts, head_of.T, queries, key_rows, value_rows, out_weight)
    projected, saved_rows = pl.pallas_call(
        hand_over,
        out_shape=(
            jax.ShapeDtypeStruct(projected.shape, projected.dtype),
            jax.ShapeDtypeStruct(saved_rows.shape, saved_rows.dtype),
        ),
        in_specs=[vmem, vmem],
        out_specs=(vmem, vmem),
        name="hand_over",
    )(
        pltpu.with_memory_space_constraint(projected, pltpu.VMEM),
        pltpu.with_memory_space_constraint(saved_rows, pltpu.VMEM),
    )
    return projected, jnp.swapaxes(saved_rows, 1, 2)[None, None]


def choose_plan(seq_count, branches, queries, key_rows, value_rows, counts, head_of, out_weight):
    operands = (queries, key_rows, value_rows, counts, head_of, out_weight)
    tokens = seq_count * queries.shape[1]
    small = tokens == LANES and queries.shape[1] % 16 == 0
    whole_turns = seq_count % 2 == 0 and HEADS % max(1, seq_count // 2) == 0
    if branches == 2 and small and whole_turns and HEADS % 2 == 0:
        return fused(seq_count, branches, *operands)
    return per_device(*operands)


def solution(mesh):
    return jax.shard_map(
        functools.partial(choose_plan, mesh.shape["seq"], mesh.shape["branch"]),
        mesh=mesh,
        in_specs=(
            P("branch", ("groups", "seq"), None),
            P("branch", ("groups", "seq"), None),
            P("branch", ("groups", "seq"), None),
            P("groups"),
            P(),
            P(None, "branch"),
        ),
        out_specs=(
            P(("groups", "seq"), "branch"),
            P("branch", ("groups", "seq"), None, None, None),
        ),
        check_vma=False,
    )
```
